512 devices in a mesh: chain: 128 (over z, y, core), seg: 4 (over x).
Axes of the slice: x: 4, y: 4, z: 16, core: 2. Of those that a mesh axis runs over, the one named last changes fastest.
Arguments:
- band_tiles: bfloat16 [128, 1024, 7, 1024], P('chain', None, None, 'seg'), may hold values from -0.009765625 to 0.009765625
- widths: int32 [128], P('chain'), may hold values from 2 to 6, as said below
- warm_start: float32 [131072, 256], P(('chain', 'seg')), may hold values from -4 to 4
- scores: float32 [131072, 64], P(('chain', 'seg')), may hold values from -6 to 6
- penalty: float32 [256], replicated, may hold values from 0.05 to 0.5
Outputs:
- fitted_effects: float32 [131072, 256], P(('chain', 'seg'))
The draws below stay inside these ranges and needn't reach their ends.
Inputs may be any that keep to these rules, and one draw needn't show every extreme that they name: `widths`: each block uses between 2 and 6 forward tiles; both 2 and 6 occur in every draw.
All inputs are finite; a program needn't handle non-finite values.
Results may differ from the reference program's by a relative error of at most 0.00085.
Values may be sent and summed in bfloat16 or wider, within the bound.
No kernel may reach another device: no remote copies, remote signals or barrier semaphores. Data moves between devices by JAX's collectives and lax.ppermute only.
A program may use at most 64 MiB of HBM per device.

```python
import math
import jax
import jax.numpy as jnp
from jax import lax

BLOCK = 1024
BAND = 6
TRAITS = 64
PATH = 4
ITERS = 2
NBLK = 128
COLS = 256


def draw_widths(key, part):
    chosen = jax.random.randint(jax.random.fold_in(key, 11), (NBLK,), 2, BAND + 1)
    ranking = jax.random.permutation(jax.random.fold_in(key, 12), NBLK)
    chosen = chosen.at[ranking[0]].set(BAND)
    chosen = chosen.at[ranking[1]].set(2)
    return chosen.astype(jnp.int32)


def level_of(rng, dims, shards, low, high):
    level = 1.0
    for dim, blocks in shards:
        draws = jax.random.uniform(jax.random.fold_in(jax.random.fold_in(rng, 6), dim), (blocks,), jnp.float32, low / len(shards), high / len(shards))
        level = level * jnp.repeat(jnp.exp(draws), dims[dim] // blocks).reshape((-1,) + (1,) * (len(dims) - 1 - dim))
    return level


def scatter_about(stream_key, extent, spread, reach, split=(), held_as=jnp.bfloat16):
    level = level_of(stream_key, extent, split, -0.22, 0.18) if split else 1.0
    values = jax.random.normal(stream_key, extent, jnp.float32) * spread * level
    return jnp.minimum(jnp.maximum(values, -reach), reach).astype(held_as)


def setup_inputs(seed: int = 0) -> dict:
    splits = jax.random.split(jax.random.key(seed), 6)
    return {
        "band_tiles": scatter_about(splits[0], (NBLK, BLOCK, BAND + 1, BLOCK), (416 * BLOCK) ** -0.5, 0.009765625, ((0, 128), (3, 4))),
        "widths": draw_widths(jax.random.fold_in(splits[5], 71), 0),
        "warm_start": scatter_about(splits[2], (NBLK * BLOCK, COLS), 0.5, 4.0, ((0, 512),), jnp.float32),
        "scores": scatter_about(splits[3], (NBLK * BLOCK, TRAITS), 1.0, 6.0, ((0, 512),), jnp.float32),
        "penalty": jnp.clip(jnp.exp(jax.random.uniform(splits[4], (COLS,), jnp.float32, math.log(0.05), math.log(0.5))), 0.05, 0.5),
    }


step_size = 0.8


def soft_limit(values, limit):
    return jnp.sign(values) * jnp.maximum(jnp.abs(values) - limit, 0.0)


def apply_band(band_tiles, widths, estimate):
    columns = estimate.shape[1]
    blocks = estimate.astype(jnp.bfloat16).reshape(NBLK, BLOCK, columns)
    zero_pad = jnp.zeros((BAND, BLOCK, columns), jnp.bfloat16)
    padded = jnp.concatenate([zero_pad, blocks, zero_pad], axis=0)
    offsets = jnp.arange(BAND + 1, dtype=jnp.int32)
    widths = widths.astype(jnp.int32)

    def one_block(block_index):
        tile_block = band_tiles[block_index].astype(jnp.float32)
        forward_blocks = lax.dynamic_slice_in_dim(padded, (block_index + BAND).astype(jnp.int32), BAND + 1, 0).astype(jnp.float32)
        live_mask = (offsets <= widths[block_index]).astype(jnp.float32)
        forward = jnp.einsum("ijk,jkc,j->ic", tile_block, forward_blocks, live_mask, precision=lax.Precision.HIGHEST)
        backward = jnp.zeros((BLOCK, columns), jnp.float32)
        for shift_by in range(BAND + 1):
            source = (block_index - shift_by).astype(jnp.int32)
            clamped = jnp.maximum(source, 0).astype(jnp.int32)
            source_tile = band_tiles[clamped][:, shift_by, :].astype(jnp.float32)
            weight = jnp.where((source >= 0) & (shift_by <= widths[clamped]), 1.0, 0.0).astype(jnp.float32)
            vector = lax.dynamic_index_in_dim(padded, (source + BAND).astype(jnp.int32), 0, keepdims=False).astype(jnp.float32)
            backward = backward + weight * jnp.dot(source_tile.T, vector, precision=lax.Precision.HIGHEST)
        return forward + backward

    result = lax.map(one_block, jnp.arange(NBLK, dtype=jnp.int32))
    return result.reshape(NBLK * BLOCK, columns)


def reference(band_tiles, widths, warm_start, scores, penalty):
    target = jnp.tile(scores, (1, PATH))
    fitted_effects = warm_start
    for iteration in range(ITERS):
        coupled = apply_band(band_tiles, widths, fitted_effects)
        stepped = fitted_effects - step_size * (fitted_effects + coupled - target)
        fitted_effects = soft_limit(stepped, step_size * penalty)
    return fitted_effects
```

```python
import functools

import jax
import jax.numpy as jnp
from jax import lax
from jax.experimental import pallas as pl
from jax.experimental.pallas import tpu as pltpu
from jax.sharding import PartitionSpec as P

ITERS = 2


step_size = 0.8

VMEM = pltpu.VMEM
F32 = jnp.float32
BF16 = jnp.bfloat16


def spec(space=None):
    return pl.BlockSpec(memory_space=VMEM if space is None else space)


def shifted(value, by):
    length = lax.axis_size("chain")
    pairs = [(i, i + by) for i in range(length) if 0 <= i + by < length]
    return lax.ppermute(value, "chain", pairs)


def swapped(value):
    length = lax.axis_size("chain")
    return lax.ppermute(value, "chain", [(i, i ^ 1) for i in range(length)])


def soft_limit(values, limit):
    return jnp.maximum(values - limit, 0.0) + jnp.minimum(values + limit, 0.0)


def begin_kernel(warm_ref, est_ref, cur_ref, copies_ref):
    est = warm_ref[...].T
    est_ref[...] = est
    cur = est.astype(BF16)
    cur_ref[...] = cur
    for s in range(copies_ref.shape[0]):
        copies_ref[s] = cur


def load_tiles(tiles_ref, held, sems):
    copies = [
        pltpu.make_async_copy(tiles_ref.at[j], held.at[j], sems.at[j])
        for j in range(held.shape[0])
    ]
    for copy in copies:
        copy.start()
    return copies


def backward_kernel(widths_ref, tiles_ref, block_ref, first_ref, rest_ref, held, sems):
    copies = load_tiles(tiles_ref, held, sems)
    n_seg, _, strip = block_ref.shape
    for j, copy in enumerate(copies):
        copy.wait()
        total = None
        for s in range(n_seg):
            term = jnp.dot(
                block_ref[s],
                held[j, pl.ds(s * strip, strip), :],
                preferred_element_type=F32,
            )
            total = term if total is None else total + term
        total = jnp.where(j <= widths_ref[0], total, 0.0)
        if j == 0:
            first_ref[...] = total
        else:
            rest_ref[j - 1] = total.astype(BF16)


def forward_kernel(
    widths_ref, tiles_ref, cur_ref, swap_ref, r1_ref, r2_ref, r3_ref, out_ref, held, total, sems
):
    copies = load_tiles(tiles_ref, held, sems)
    n_seg = out_ref.shape[0]
    strip = out_ref.shape[2]
    ahead = [
        lambda: cur_ref[...],
        lambda: swap_ref[0],
        lambda: r1_ref[...],
        lambda: swap_ref[1],
        lambda: r2_ref[...],
        lambda: swap_ref[2],
        lambda: r3_ref[...],
    ]
    for j, copy in enumerate(copies):
        copy.wait()
        value = ahead[j]()
        value = jnp.where(j <= widths_ref[0], value, jnp.zeros_like(value))
        for s in range(n_seg):
            term = lax.dot_general(
                value,
                held[j, pl.ds(s * strip, strip), :],
                (((1,), (1,)), ((), ())),
                preferred_element_type=F32,
            )
            if j == 0:
                total[s] = term
            elif j < len(copies) - 1:
                total[s] += term
            else:
                out_ref[s] = (total[s] + term).astype(BF16)


def new_estimate(odd_ref, est_ref, first_ref, pair_ref, seg_ref, b1_ref, b2_ref, b3_ref, scores_ref, pen_ref):
    coupled = first_ref[...]
    pair = pair_ref[0].astype(F32)
    coupled = coupled + jnp.where(odd_ref[0] == 1, pair, 0.0)
    for s in range(seg_ref.shape[0]):
        coupled = coupled + seg_ref[s].astype(F32)
    for ref in (b1_ref, b2_ref, b3_ref):
        coupled = coupled + ref[...].astype(F32)
    est = est_ref[...]
    columns, traits = est.shape[0], scores_ref.shape[0]
    target = jnp.concatenate([scores_ref[...]] * (columns // traits), axis=0)
    stepped = est - step_size * (est + coupled - target)
    return soft_limit(stepped, pen_ref[...])


def update_kernel(*refs):
    new_ref, cur_ref, copies_ref = refs[-3:]
    est = new_estimate(*refs[:-3])
    new_ref[...] = est
    cur = est.astype(BF16)
    cur_ref[...] = cur
    for s in range(copies_ref.shape[0]):
        copies_ref[s] = cur


def final_kernel(*refs):
    refs[-1][...] = new_estimate(*refs[:-1]).T


def per_device(band_tiles, widths, warm_start, scores, penalty):
    n_seg = lax.axis_size("seg")
    tiles = jnp.transpose(band_tiles[0], (1, 0, 2))
    depth, block_len, strip = tiles.shape
    columns = warm_start.shape[1]
    scores_t = scores.T
    pen = jnp.broadcast_to((step_size * penalty)[:, None], (columns, strip))
    odd = lax.rem(lax.axis_index("chain"), 2).astype(jnp.int32)
    is_odd = odd == 1
    odd_arr = odd.reshape((1,))
    vec_f32 = jax.ShapeDtypeStruct((columns, strip), F32)
    vec_bf16 = jax.ShapeDtypeStruct((columns, strip), BF16)
    seg_bf16 = jax.ShapeDtypeStruct((n_seg, columns, strip), BF16)
    smem = spec(pltpu.SMEM)
    hbm = spec(pl.ANY)
    flops = 2 * depth * block_len * strip * columns
    mat_cost = pl.CostEstimate(
        flops=flops, bytes_accessed=depth * block_len * strip * 2, transcendentals=0
    )
    small_cost = pl.CostEstimate(
        flops=20 * columns * strip, bytes_accessed=12 * columns * strip, transcendentals=0
    )
    tile_scratch = [VMEM((depth, block_len, strip), BF16)]
    tile_sems = [pltpu.SemaphoreType.DMA((depth,))]

    begin = pl.pallas_call(
        begin_kernel,
        out_shape=(vec_f32, vec_bf16, seg_bf16),
        in_specs=[spec()],
        out_specs=(spec(),) * 3,
        cost_estimate=small_cost,
        compiler_params=pltpu.CompilerParams(vmem_limit_bytes=4 << 20),
        name="begin",
    )
    backward = pl.pallas_call(
        backward_kernel,
        out_shape=(vec_f32, jax.ShapeDtypeStruct((depth - 1, columns, strip), BF16)),
        in_specs=[smem, hbm, spec()],
        out_specs=(spec(),) * 2,
        scratch_shapes=tile_scratch + tile_sems,
        cost_estimate=mat_cost,
        compiler_params=pltpu.CompilerParams(vmem_limit_bytes=10 << 20),
        name="backward",
    )
    forward = pl.pallas_call(
        forward_kernel,
        out_shape=seg_bf16,
        in_specs=[smem, hbm] + [spec()] * 5,
        out_specs=spec(),
        scratch_shapes=tile_scratch + [VMEM((n_seg, columns, strip), F32)] + tile_sems,
        cost_estimate=mat_cost,
        compiler_params=pltpu.CompilerParams(vmem_limit_bytes=10 << 20),
        name="forward",
    )
    update = pl.pallas_call(
        update_kernel,
        out_shape=(vec_f32, vec_bf16, seg_bf16),
        in_specs=[smem] + [spec()] * 9,
        out_specs=(spec(),) * 3,
        cost_estimate=small_cost,
        compiler_params=pltpu.CompilerParams(vmem_limit_bytes=8 << 20),
        name="update",
    )
    final = pl.pallas_call(
        final_kernel,
        out_shape=jax.ShapeDtypeStruct((strip, columns), F32),
        in_specs=[smem] + [spec()] * 9,
        out_specs=spec(),
        cost_estimate=small_cost,
        compiler_params=pltpu.CompilerParams(vmem_limit_bytes=8 << 20),
        name="final",
    )

    estimate, current, copies = begin(warm_start)
    for iteration in range(ITERS):
        block = lax.all_to_all(copies, "seg", 0, 0)
        r3, r2, r1 = (shifted(current, -2 * k) for k in (3, 2, 1))
        first, rest = backward(widths, tiles, block)
        lent = jnp.stack(
            [
                jnp.where(is_odd, current, r1),
                jnp.where(is_odd, r1, r2),
                jnp.where(is_odd, r2, r3),
                rest[0],
                rest[2],
                rest[4],
            ]
        )
        got = swapped(lent)
        add_1 = jnp.where(is_odd, got[4], got[3]).astype(F32)
        add_2 = jnp.where(is_odd, got[5], got[4]).astype(F32)
        add_3 = jnp.where(is_odd, jnp.zeros_like(got[5]), got[5]).astype(F32)
        t1 = (rest[1].astype(F32) + add_1).astype(BF16)
        t2 = (rest[3].astype(F32) + add_2).astype(BF16)
        t3 = (rest[5].astype(F32) + add_3).astype(BF16)
        partial = forward(widths, tiles, current, got, r1, r2, r3)
        summed = lax.all_to_all(partial, "seg", 0, 0)
        b3, b2, b1 = shifted(t3, 6), shifted(t2, 4), shifted(t1, 2)
        operands = (odd_arr, estimate, first, got[3:4], summed, b1, b2, b3, scores_t, pen)
        if iteration < ITERS - 1:
            estimate, current, copies = update(*operands)
        else:
            return final(*operands)


def solution(mesh):
    in_specs = (
        P("chain", None, None, "seg"),
        P("chain"),
        P(("chain", "seg"), None),
        P(("chain", "seg"), None),
        P(),
    )
    out_specs = P(("chain", "seg"), None)
    return jax.shard_map(
        per_device, mesh=mesh, in_specs=in_specs, out_specs=out_specs, check_vma=False
    )
```

```python
import jax
import jax.numpy as jnp
from jax import lax
from jax.experimental import pallas as pl
from jax.experimental.pallas import tpu as pltpu
from jax.sharding import PartitionSpec as P


ITERS = 2


step_size = 0.8

VMEM = pltpu.VMEM
HBM = pltpu.HBM
F32 = jnp.float32
BF16 = jnp.bfloat16


def spec(space=None):
    return pl.BlockSpec(memory_space=VMEM if space is None else space)


def shifted(value, by):
    length = lax.axis_size("chain")
    pairs = [(i, i + by) for i in range(length) if 0 <= i + by < length]
    return lax.ppermute(value, "chain", pairs)


def swapped(value):
    length = lax.axis_size("chain")
    return lax.ppermute(value, "chain", [(i, i ^ 1) for i in range(length)])


def soft_limit(values, limit):
    return jnp.maximum(values - limit, 0.0) + jnp.minimum(values + limit, 0.0)


def begin_kernel(warm_ref, est_ref, cur_ref, copies_ref):
    est = warm_ref[...].T
    est_ref[...] = est
    cur = est.astype(BF16)
    cur_ref[...] = cur
    for s in range(copies_ref.shape[0]):
        copies_ref[s] = cur


def pair_kernel(cur_ref, far_ref, out_ref):
    out_ref[0] = cur_ref[...]
    out_ref[1] = far_ref[...]


def backward_body(widths_ref, held, block_ref, first_ref, even_ref, lent_ref, wait):
    block = jnp.concatenate([block_ref[s] for s in range(block_ref.shape[0])], axis=1)
    for j in range(held.shape[0]):
        wait(j)
        total = jnp.dot(block, held[j], preferred_element_type=F32)
        total = jnp.where(j <= widths_ref[0], total, 0.0)
        if j == 0:
            first_ref[...] = total
        elif j % 2 == 0:
            even_ref[j // 2 - 1] = total.astype(BF16)
        else:
            lent_ref[3 + j // 2] = total.astype(BF16)


def backward_load_kernel(widths_ref, tiles_ref, block_ref, first_ref, even_ref, lent_ref, held, sems):
    copies = [
        pltpu.make_async_copy(tiles_ref.at[j], held.at[j], sems.at[j])
        for j in range(held.shape[0])
    ]
    for copy in copies:
        copy.start()
    backward_body(
        widths_ref, held, block_ref, first_ref, even_ref, lent_ref, lambda j: copies[j].wait()
    )


def backward_kernel(widths_ref, held, block_ref, first_ref, even_ref, lent_ref):
    backward_body(widths_ref, held, block_ref, first_ref, even_ref, lent_ref, lambda j: None)


def lend_kernel(odd_ref, lent_ref, cur_ref, near_ref, far_ref, out_ref):
    del lent_ref

    @pl.when(odd_ref[0] == 1)
    def _():
        out_ref[0] = cur_ref[...]
        out_ref[1] = near_ref[0]
        out_ref[2] = far_ref[...]

    @pl.when(odd_ref[0] == 0)
    def _():
        out_ref[0] = near_ref[0]
        out_ref[1] = far_ref[...]
        out_ref[2] = near_ref[1]


def forward_product(widths_ref, held, values, offsets, s):
    strip = held.shape[2]
    left = jnp.concatenate(
        [jnp.where(j <= widths_ref[0], v, jnp.zeros_like(v)) for j, v in zip(offsets, values)],
        axis=1,
    )
    right = jnp.concatenate([held[j, pl.ds(s * strip, strip), :] for j in offsets], axis=1)
    return lax.dot_general(left, right, (((1,), (1,)), ((), ())), preferred_element_type=F32)


def forward_even_kernel(widths_ref, held, cur_ref, near_ref, far_ref, total_ref):
    values = [cur_ref[...], near_ref[0], far_ref[...], near_ref[1]]
    for s in range(total_ref.shape[0]):
        total_ref[s] = forward_product(widths_ref, held, values, (0, 2, 4, 6), s)


def forward_odd_kernel(widths_ref, held, got_ref, total_ref, out_ref):
    values = [got_ref[0], got_ref[1], got_ref[2]]
    for s in range(out_ref.shape[0]):
        term = forward_product(widths_ref, held, values, (1, 3, 5), s)
        out_ref[s] = (total_ref[s] + term).astype(BF16)


def combine_kernel(odd_ref, even_ref, got_ref, pair_ref, mid_ref):
    def add(k, other):
        return (even_ref[k].astype(F32) + other.astype(F32)).astype(BF16)

    @pl.when(odd_ref[0] == 1)
    def _():
        pair_ref[0] = add(0, got_ref[4])
        mid_ref[...] = add(1, got_ref[5])
        pair_ref[1] = even_ref[2]

    @pl.when(odd_ref[0] == 0)
    def _():
        pair_ref[0] = add(0, got_ref[3])
        mid_ref[...] = add(1, got_ref[4])
        pair_ref[1] = add(2, got_ref[5])


def relay_kernel(mid_ref, near_ref, out_ref):
    out_ref[...] = (mid_ref[...].astype(F32) + near_ref[1].astype(F32)).astype(BF16)


def new_estimate(odd_ref, est_ref, first_ref, got_ref, seg_ref, near_ref, far_ref, scores_ref, pen_ref):
    coupled = first_ref[...]
    coupled = coupled + jnp.where(odd_ref[0] == 1, got_ref[3].astype(F32), 0.0)
    for s in range(seg_ref.shape[0]):
        coupled = coupled + seg_ref[s].astype(F32)
    coupled = coupled + near_ref[0].astype(F32)
    coupled = coupled + far_ref[...].astype(F32)
    est = est_ref[...]
    columns, traits = est.shape[0], scores_ref.shape[0]
    target = jnp.concatenate([scores_ref[...]] * (columns // traits), axis=0)
    stepped = est - step_size * (est + coupled - target)
    return soft_limit(stepped, pen_ref[...])


def update_kernel(*refs):
    new_ref, cur_ref, copies_ref = refs[-3:]
    est = new_estimate(*refs[:-3])
    new_ref[...] = est
    cur = est.astype(BF16)
    cur_ref[...] = cur
    for s in range(copies_ref.shape[0]):
        copies_ref[s] = cur


def final_kernel(*refs):
    refs[-1][...] = new_estimate(*refs[:-1]).T


def call(kernel, out_shape, n_in, scalars, flops, nbytes, mib, tiles_in=None, **more):
    ins = [spec(pltpu.SMEM)] * scalars + [spec()] * (n_in - scalars)
    if tiles_in is not None:
        ins[tiles_in] = spec(HBM)
    outs = jax.tree.map(lambda _: spec(), out_shape)
    return pl.pallas_call(
        kernel,
        out_shape=out_shape,
        in_specs=ins,
        out_specs=outs,
        cost_estimate=pl.CostEstimate(flops=flops, bytes_accessed=nbytes, transcendentals=0),
        compiler_params=pltpu.CompilerParams(vmem_limit_bytes=mib << 20),
        **more,
    )


def per_device(band_tiles, widths, warm_start, scores, penalty):
    n_seg = lax.axis_size("seg")
    tiles = pltpu.with_memory_space_constraint(jnp.transpose(band_tiles[0], (1, 0, 2)), HBM)
    depth, block_len, strip = tiles.shape
    columns = warm_start.shape[1]
    scores_t = scores.T
    pen = jnp.broadcast_to((step_size * penalty)[:, None], (columns, strip))
    odd = lax.rem(lax.axis_index("chain"), 2).astype(jnp.int32).reshape((1,))

    def shape(dtype, *lead):
        return jax.ShapeDtypeStruct((*lead, columns, strip), dtype)

    flops = 2 * depth * block_len * strip * columns
    tile_bytes = depth * block_len * strip * 2
    one = columns * strip
    begin = call(begin_kernel, (shape(F32), shape(BF16), shape(BF16, n_seg)), 1, 0, one, 8 * one, 4)
    pair = call(pair_kernel, shape(BF16, 2), 2, 0, one, 8 * one, 2)
    products = (shape(F32), shape(BF16, 3), shape(BF16, 6))
    backward_load = call(
        backward_load_kernel,
        (*products, VMEM(tiles.shape, BF16)),
        3,
        1,
        flops,
        tile_bytes,
        8,
        tiles_in=1,
        scratch_shapes=[pltpu.SemaphoreType.DMA((depth,))],
    )
    backward = call(backward_kernel, products, 3, 1, flops, tile_bytes, 8)
    lend = call(lend_kernel, shape(BF16, 6), 5, 1, one, 12 * one, 4, input_output_aliases={1: 0})
    forward_even = call(forward_even_kernel, shape(F32, n_seg), 5, 1, flops * 4 // 7, tile_bytes, 8)
    forward_odd = call(forward_odd_kernel, shape(BF16, n_seg), 4, 1, flops * 3 // 7, tile_bytes, 8)
    combine = call(combine_kernel, (shape(BF16, 2), shape(BF16)), 3, 1, one, 18 * one, 4)
    relay = call(relay_kernel, shape(BF16), 2, 0, one, 6 * one, 2)
    update = call(update_kernel, (shape(F32), shape(BF16), shape(BF16, n_seg)), 9, 1, one, 12 * one, 8)
    final = call(final_kernel, jax.ShapeDtypeStruct((strip, columns), F32), 9, 1, one, 12 * one, 8)

    estimate, current, copies = begin(warm_start)
    for iteration in range(ITERS):
        far = shifted(current, -4)
        block = lax.all_to_all(copies, "seg", 0, 0)
        near = shifted(pair(current, far), -2)
        if iteration == 0:
            first, even, lent, held = backward_load(widths, tiles, block)
        else:
            first, even, lent = backward(widths, held, block)
        got = swapped(lend(odd, lent, current, near, far))
        total = forward_even(widths, held, current, near, far)
        back_pair, mid = combine(odd, even, got)
        back_near = shifted(back_pair, 2)
        partial = forward_odd(widths, held, got, total)
        summed = lax.all_to_all(partial, "seg", 0, 0)
        back_far = shifted(relay(mid, back_near), 4)
        operands = (odd, estimate, first, got, summed, back_near, back_far, scores_t, pen)
        if iteration < ITERS - 1:
            estimate, current, copies = update(*operands)
        else:
            return final(*operands)


def solution(mesh):
    in_specs = (
        P("chain", None, None, "seg"),
        P("chain"),
        P(("chain", "seg"), None),
        P(("chain", "seg"), None),
        P(),
    )
    out_specs = P(("chain", "seg"), None)
    return jax.shard_map(
        per_device, mesh=mesh, in_specs=in_specs, out_specs=out_specs, check_vma=False
    )
```

```python
import jax
import jax.numpy as jnp
from jax import lax
from jax.experimental import pallas as pl
from jax.experimental.pallas import tpu as pltpu
from jax.sharding import PartitionSpec as P


ITERS = 2
EARLY = 2


step_size = 0.8

VMEM = pltpu.VMEM
HBM = pltpu.HBM
F32 = jnp.float32
BF16 = jnp.bfloat16


def spec(space=None):
    return pl.BlockSpec(memory_space=VMEM if space is None else space)


def shifted(value, by):
    length = lax.axis_size("chain")
    pairs = [(i, i + by) for i in range(length) if 0 <= i + by < length]
    return lax.ppermute(value, "chain", pairs)


def swapped(value):
    length = lax.axis_size("chain")
    return lax.ppermute(value, "chain", [(i, i ^ 1) for i in range(length)])


def is_odd():
    return lax.rem(lax.axis_index("chain"), 2) == 1


def soft_limit(values, limit):
    return jnp.maximum(values - limit, 0.0) + jnp.minimum(values + limit, 0.0)


def send_copies(cur_ref, copies_ref, sems):
    copies = [
        pltpu.make_async_copy(cur_ref, copies_ref.at[s], sems.at[s])
        for s in range(copies_ref.shape[0])
    ]
    for copy in copies:
        copy.start()
    return copies


def begin_kernel(warm_ref, est_ref, cur_ref, copies_ref, held, in_sems, out_sems):
    parts, rows, _ = held.shape
    loads = [
        pltpu.make_async_copy(warm_ref.at[pl.ds(i * rows, rows), :], held.at[i], in_sems.at[i])
        for i in range(parts)
    ]
    for load in loads:
        load.start()
    for i, load in enumerate(loads):
        load.wait()
        est = held[i].T
        est_ref[:, i * rows : (i + 1) * rows] = est
        cur_ref[:, i * rows : (i + 1) * rows] = est.astype(BF16)
    for copy in send_copies(cur_ref, copies_ref, out_sems):
        copy.wait()


def pair_kernel(cur_ref, far_ref, out_ref):
    out_ref[0] = cur_ref[...]
    out_ref[1] = far_ref[...]


def load_kernel(tiles_ref, far_ref, held, sem):
    del far_ref
    copy = pltpu.make_async_copy(tiles_ref.at[pl.ds(0, EARLY)], held, sem)
    copy.start()
    copy.wait()


def backward_kernel(
    widths_ref, tiles_ref, early_ref, block_ref, first_ref, even_ref, lent_ref, late_ref, sems
):
    late = late_ref.shape[0]
    copies = [
        pltpu.make_async_copy(tiles_ref.at[EARLY + i], late_ref.at[i], sems.at[i])
        for i in range(late)
    ]
    for copy in copies:
        copy.start()
    block = jnp.concatenate([block_ref[s] for s in range(block_ref.shape[0])], axis=1)
    for j in range(EARLY + late):
        if j >= EARLY:
            copies[j - EARLY].wait()
        tile = early_ref[j] if j < EARLY else late_ref[j - EARLY]
        total = jnp.dot(block, tile, preferred_element_type=F32)
        total = jnp.where(j <= widths_ref[0], total, 0.0)
        if j == 0:
            first_ref[...] = total
        elif j % 2 == 0:
            even_ref[j // 2 - 1] = total.astype(BF16)
        else:
            lent_ref[3 + j // 2] = total.astype(BF16)


def lend_kernel(lent_ref, cur_ref, near_ref, far_ref, out_ref):
    del lent_ref

    @pl.when(is_odd())
    def _():
        out_ref[0] = cur_ref[...]
        out_ref[1] = near_ref[0]
        out_ref[2] = far_ref[...]

    @pl.when(jnp.logical_not(is_odd()))
    def _():
        out_ref[0] = near_ref[0]
        out_ref[1] = far_ref[...]
        out_ref[2] = near_ref[1]


def forward_product(widths_ref, early_ref, late_ref, values, offsets, s):
    strip = early_ref.shape[2]
    rows = pl.ds(s * strip, strip)
    left = jnp.concatenate(
        [jnp.where(j <= widths_ref[0], v, jnp.zeros_like(v)) for j, v in zip(offsets, values)],
        axis=1,
    )
    right = jnp.concatenate(
        [early_ref[j, rows, :] if j < EARLY else late_ref[j - EARLY, rows, :] for j in offsets],
        axis=1,
    )
    return lax.dot_general(left, right, (((1,), (1,)), ((), ())), preferred_element_type=F32)


def forward_even_kernel(widths_ref, early_ref, late_ref, cur_ref, near_ref, far_ref, total_ref):
    values = [cur_ref[...], near_ref[0], far_ref[...], near_ref[1]]
    for s in range(total_ref.shape[0]):
        total_ref[s] = forward_product(widths_ref, early_ref, late_ref, values, (0, 2, 4, 6), s)


def forward_odd_kernel(widths_ref, early_ref, late_ref, got_ref, total_ref, out_ref, parts, sems):
    values = [got_ref[0], got_ref[1], got_ref[2]]
    copies = []
    for s in range(out_ref.shape[0]):
        term = forward_product(widths_ref, early_ref, late_ref, values, (1, 3, 5), s)
        parts[s] = (total_ref[s] + term).astype(BF16)
        copies.append(pltpu.make_async_copy(parts.at[s], out_ref.at[s], sems.at[s]))
        copies[-1].start()
    for copy in copies:
        copy.wait()


def combine_kernel(even_ref, got_ref, pair_ref, mid_ref):
    def add(k, other):
        return (even_ref[k].astype(F32) + other.astype(F32)).astype(BF16)

    @pl.when(is_odd())
    def _():
        pair_ref[0] = add(0, got_ref[4])
        mid_ref[...] = add(1, got_ref[5])
        pair_ref[1] = even_ref[2]

    @pl.when(jnp.logical_not(is_odd()))
    def _():
        pair_ref[0] = add(0, got_ref[3])
        mid_ref[...] = add(1, got_ref[4])
        pair_ref[1] = add(2, got_ref[5])


def relay_kernel(mid_ref, near_ref, out_ref):
    out_ref[...] = (mid_ref[...].astype(F32) + near_ref[1].astype(F32)).astype(BF16)


def settle_kernel(est_ref, first_ref, got_ref, near_ref, scores_ref, out_ref):
    coupled = first_ref[...] + jnp.where(is_odd(), got_ref[3].astype(F32), 0.0)
    coupled = coupled + near_ref[0].astype(F32)
    est = est_ref[...]
    columns, traits = est.shape[0], scores_ref.shape[0]
    target = jnp.concatenate([scores_ref[...]] * (columns // traits), axis=0)
    out_ref[...] = est - step_size * (est + coupled - target)


def new_estimate(settled_ref, seg_ref, far_ref, pen_ref):
    coupled = far_ref[...].astype(F32)
    for s in range(seg_ref.shape[0]):
        coupled = coupled + seg_ref[s].astype(F32)
    return soft_limit(settled_ref[...] - step_size * coupled, pen_ref[...])


def update_kernel(settled_ref, seg_ref, far_ref, pen_ref, new_ref, cur_ref, copies_ref, sems):
    est = new_estimate(settled_ref, seg_ref, far_ref, pen_ref)
    cur_ref[...] = est.astype(BF16)
    copies = send_copies(cur_ref, copies_ref, sems)
    new_ref[...] = est
    for copy in copies:
        copy.wait()


def final_kernel(settled_ref, seg_ref, far_ref, pen_ref, out_ref):
    out_ref[...] = new_estimate(settled_ref, seg_ref, far_ref, pen_ref).T


def call(kernel, out_shape, n_in, scalars, flops, nbytes, mib, outside=(), out_outside=(), **more):
    ins = [spec(pltpu.SMEM)] * scalars + [spec()] * (n_in - scalars)
    for i in outside:
        ins[i] = spec(HBM)
    many = isinstance(out_shape, tuple)
    outs = [spec()] * (len(out_shape) if many else 1)
    for i in out_outside:
        outs[i] = spec(HBM)
    return pl.pallas_call(
        kernel,
        out_shape=out_shape,
        in_specs=ins,
        out_specs=tuple(outs) if many else outs[0],
        cost_estimate=pl.CostEstimate(flops=flops, bytes_accessed=nbytes, transcendentals=0),
        compiler_params=pltpu.CompilerParams(vmem_limit_bytes=mib << 20),
        **more,
    )


def per_device(band_tiles, widths, warm_start, scores, penalty):
    n_seg = lax.axis_size("seg")
    tiles = pltpu.with_memory_space_constraint(jnp.transpose(band_tiles[0], (1, 0, 2)), HBM)
    depth, block_len, strip = tiles.shape
    columns = warm_start.shape[1]
    scores_t = scores.T
    pen = jnp.broadcast_to((step_size * penalty)[:, None], (columns, strip))

    def shape(dtype, *lead):
        return jax.ShapeDtypeStruct((*lead, columns, strip), dtype)

    flops = 2 * depth * block_len * strip * columns
    tile_bytes = depth * block_len * strip * 2
    one = columns * strip
    seg_sems = pltpu.SemaphoreType.DMA((n_seg,))
    fresh = (shape(F32), shape(BF16), HBM((n_seg, columns, strip), BF16))
    begin = call(
        begin_kernel,
        fresh,
        1,
        0,
        one,
        8 * one,
        4,
        outside=(0,),
        out_outside=(2,),
        scratch_shapes=[VMEM((2, strip // 2, columns), F32), pltpu.SemaphoreType.DMA((2,)), seg_sems],
    )
    pair = call(pair_kernel, shape(BF16, 2), 2, 0, one, 8 * one, 2)
    load = call(
        load_kernel,
        jax.ShapeDtypeStruct((EARLY, block_len, strip), BF16),
        2,
        0,
        one,
        tile_bytes * EARLY // depth,
        4,
        outside=(0,),
        scratch_shapes=[pltpu.SemaphoreType.DMA],
    )
    backward = call(
        backward_kernel,
        (
            shape(F32),
            shape(BF16, 3),
            shape(BF16, 6),
            jax.ShapeDtypeStruct((depth - EARLY, block_len, strip), BF16),
        ),
        4,
        1,
        flops,
        tile_bytes,
        8,
        outside=(1,),
        scratch_shapes=[pltpu.SemaphoreType.DMA((depth - EARLY,))],
    )
    lend = call(lend_kernel, shape(BF16, 6), 4, 0, one, 12 * one, 4, input_output_aliases={0: 0})
    forward_even = call(forward_even_kernel, shape(F32, n_seg), 6, 1, flops * 4 // 7, tile_bytes, 8)
    forward_odd = call(
        forward_odd_kernel,
        HBM((n_seg, columns, strip), BF16),
        5,
        1,
        flops * 3 // 7,
        tile_bytes,
        8,
        out_outside=(0,),
        scratch_shapes=[VMEM((n_seg, columns, strip), BF16), seg_sems],
    )
    combine = call(combine_kernel, (shape(BF16, 2), shape(BF16)), 2, 0, one, 18 * one, 4)
    relay = call(relay_kernel, shape(BF16), 2, 0, one, 6 * one, 2)
    settle = call(settle_kernel, shape(F32), 5, 0, one, 14 * one, 4)
    update = call(
        update_kernel, fresh, 4, 0, one, 12 * one, 6, out_outside=(2,), scratch_shapes=[seg_sems]
    )
    final = call(final_kernel, jax.ShapeDtypeStruct((strip, columns), F32), 4, 0, one, 12 * one, 6)

    estimate, current, copies = begin(pltpu.with_memory_space_constraint(warm_start, HBM))
    for iteration in range(ITERS):
        far = shifted(current, -4)
        block = lax.all_to_all(copies, "seg", 0, 0)
        near = shifted(pair(current, far), -2)
        early = load(tiles, far)
        first, even, lent, late = backward(widths, tiles, early, block)
        got = swapped(lend(lent, current, near, far))
        total = forward_even(widths, early, late, current, near, far)
        back_pair, mid = combine(even, got)
        back_near = shifted(back_pair, 2)
        partial = forward_odd(widths, early, late, got, total)
        summed = lax.all_to_all(partial, "seg", 0, 0)
        back_far = shifted(relay(mid, back_near), 4)
        settled = settle(estimate, first, got, back_near, scores_t)
        if iteration < ITERS - 1:
            estimate, current, copies = update(settled, summed, back_far, pen)
        else:
            return final(settled, summed, back_far, pen)


def solution(mesh):
    in_specs = (
        P("chain", None, None, "seg"),
        P("chain"),
        P(("chain", "seg"), None),
        P(("chain", "seg"), None),
        P(),
    )
    out_specs = P(("chain", "seg"), None)
    return jax.shard_map(
        per_device, mesh=mesh, in_specs=in_specs, out_specs=out_specs, check_vma=False
    )
```

```python
import jax
import jax.numpy as jnp
from jax import lax
from jax.experimental import pallas as pl
from jax.experimental.pallas import tpu as pltpu
from jax.sharding import PartitionSpec as P


ITERS = 2
EARLY = 2


step_size = 0.8

VMEM = pltpu.VMEM
HBM = pltpu.HBM
F32 = jnp.float32
BF16 = jnp.bfloat16


def spec(space=None):
    return pl.BlockSpec(memory_space=VMEM if space is None else space)


def shifted(value, by):
    length = lax.axis_size("chain")
    pairs = [(i, i + by) for i in range(length) if 0 <= i + by < length]
    return lax.ppermute(value, "chain", pairs)


def swapped(value):
    length = lax.axis_size("chain")
    return lax.ppermute(value, "chain", [(i, i ^ 1) for i in range(length)])


def is_odd():
    return lax.rem(lax.axis_index("chain"), 2) == 1


def soft_limit(values, limit):
    return jnp.maximum(values - limit, 0.0) + jnp.minimum(values + limit, 0.0)


def send_copies(cur_ref, copies_ref, sems):
    copies = [
        pltpu.make_async_copy(cur_ref, copies_ref.at[s], sems.at[s])
        for s in range(copies_ref.shape[0])
    ]
    for copy in copies:
        copy.start()
    return copies


def begin_kernel(warm_ref, est_ref, cur_ref, held, in_sems):
    parts, rows, _ = held.shape
    loads = [
        pltpu.make_async_copy(warm_ref.at[pl.ds(i * rows, rows), :], held.at[i], in_sems.at[i])
        for i in range(parts)
    ]
    for load in loads:
        load.start()
    for i, load in enumerate(loads):
        load.wait()
        est = held[i].T
        est_ref[:, i * rows : (i + 1) * rows] = est
        cur_ref[:, i * rows : (i + 1) * rows] = est.astype(BF16)


def spread_kernel(cur_ref, copies_ref, sems):
    for copy in send_copies(cur_ref, copies_ref, sems):
        copy.wait()


def pair_kernel(cur_ref, far_ref, out_ref):
    out_ref[0] = cur_ref[...]
    out_ref[1] = far_ref[...]


def load_kernel(tiles_ref, far_ref, held, sem):
    del far_ref
    copy = pltpu.make_async_copy(tiles_ref.at[pl.ds(0, EARLY)], held, sem)
    copy.start()
    copy.wait()


def backward_kernel(
    widths_ref, tiles_ref, early_ref, block_ref, first_ref, even_ref, lent_ref, late_ref, sems
):
    late = late_ref.shape[0]
    copies = [
        pltpu.make_async_copy(tiles_ref.at[EARLY + i], late_ref.at[i], sems.at[i])
        for i in range(late)
    ]
    for copy in copies:
        copy.start()
    block = jnp.concatenate([block_ref[s] for s in range(block_ref.shape[0])], axis=1)
    for j in range(EARLY + late):
        if j >= EARLY:
            copies[j - EARLY].wait()
        tile = early_ref[j] if j < EARLY else late_ref[j - EARLY]
        total = jnp.dot(block, tile, preferred_element_type=F32)
        total = jnp.where(j <= widths_ref[0], total, 0.0)
        if j == 0:
            first_ref[...] = total
        elif j % 2 == 0:
            even_ref[j // 2 - 1] = total.astype(BF16)
        else:
            lent_ref[3 + j // 2] = total.astype(BF16)


def lend_kernel(lent_ref, cur_ref, near_ref, far_ref, out_ref):
    del lent_ref

    @pl.when(is_odd())
    def _():
        out_ref[0] = cur_ref[...]
        out_ref[1] = near_ref[0]
        out_ref[2] = far_ref[...]

    @pl.when(jnp.logical_not(is_odd()))
    def _():
        out_ref[0] = near_ref[0]
        out_ref[1] = far_ref[...]
        out_ref[2] = near_ref[1]


def forward_product(widths_ref, early_ref, late_ref, values, offsets, s):
    strip = early_ref.shape[2]
    rows = pl.ds(s * strip, strip)
    left = jnp.concatenate(
        [jnp.where(j <= widths_ref[0], v, jnp.zeros_like(v)) for j, v in zip(offsets, values)],
        axis=1,
    )
    right = jnp.concatenate(
        [early_ref[j, rows, :] if j < EARLY else late_ref[j - EARLY, rows, :] for j in offsets],
        axis=1,
    )
    return lax.dot_general(left, right, (((1,), (1,)), ((), ())), preferred_element_type=F32)


def forward_even_kernel(widths_ref, early_ref, late_ref, cur_ref, near_ref, far_ref, total_ref):
    values = [cur_ref[...], near_ref[0], far_ref[...], near_ref[1]]
    for s in range(total_ref.shape[0]):
        total_ref[s] = forward_product(widths_ref, early_ref, late_ref, values, (0, 2, 4, 6), s)


def forward_odd_kernel(widths_ref, early_ref, late_ref, got_ref, total_ref, out_ref, parts, sems):
    values = [got_ref[0], got_ref[1], got_ref[2]]
    copies = []
    for s in range(out_ref.shape[0]):
        term = forward_product(widths_ref, early_ref, late_ref, values, (1, 3, 5), s)
        parts[s] = (total_ref[s] + term).astype(BF16)
        copies.append(pltpu.make_async_copy(parts.at[s], out_ref.at[s], sems.at[s]))
        copies[-1].start()
    for copy in copies:
        copy.wait()


def combine_kernel(even_ref, got_ref, pair_ref, mid_ref):
    def add(k, other):
        return (even_ref[k].astype(F32) + other.astype(F32)).astype(BF16)

    @pl.when(is_odd())
    def _():
        mid_ref[...] = add(0, got_ref[4])
        pair_ref[0] = add(1, got_ref[5])
        pair_ref[1] = even_ref[2]

    @pl.when(jnp.logical_not(is_odd()))
    def _():
        mid_ref[...] = add(0, got_ref[3])
        pair_ref[0] = add(1, got_ref[4])
        pair_ref[1] = add(2, got_ref[5])


def relay_kernel(mid_ref, near_ref, out_ref):
    out_ref[...] = (mid_ref[...].astype(F32) + near_ref[1].astype(F32)).astype(BF16)


def settle_kernel(est_ref, first_ref, got_ref, near_ref, scores_ref, out_ref):
    coupled = first_ref[...] + jnp.where(is_odd(), got_ref[3].astype(F32), 0.0)
    coupled = coupled + near_ref[0].astype(F32)
    est = est_ref[...]
    columns, traits = est.shape[0], scores_ref.shape[0]
    target = jnp.concatenate([scores_ref[...]] * (columns // traits), axis=0)
    out_ref[...] = est - step_size * (est + coupled - target)


def new_estimate(settled_ref, seg_ref, far_ref, pen_ref):
    coupled = far_ref[...].astype(F32)
    for s in range(seg_ref.shape[0]):
        coupled = coupled + seg_ref[s].astype(F32)
    return soft_limit(settled_ref[...] - step_size * coupled, pen_ref[...])


def update_kernel(settled_ref, seg_ref, far_ref, pen_ref, new_ref, cur_ref):
    est = new_estimate(settled_ref, seg_ref, far_ref, pen_ref)
    cur_ref[...] = est.astype(BF16)
    new_ref[...] = est


def final_kernel(settled_ref, seg_ref, far_ref, pen_ref, out_ref):
    out_ref[...] = new_estimate(settled_ref, seg_ref, far_ref, pen_ref).T


def call(kernel, out_shape, n_in, scalars, flops, nbytes, mib, outside=(), out_outside=(), **more):
    ins = [spec(pltpu.SMEM)] * scalars + [spec()] * (n_in - scalars)
    for i in outside:
        ins[i] = spec(HBM)
    many = isinstance(out_shape, tuple)
    outs = [spec()] * (len(out_shape) if many else 1)
    for i in out_outside:
        outs[i] = spec(HBM)
    return pl.pallas_call(
        kernel,
        out_shape=out_shape,
        in_specs=ins,
        out_specs=tuple(outs) if many else outs[0],
        cost_estimate=pl.CostEstimate(flops=flops, bytes_accessed=nbytes, transcendentals=0),
        compiler_params=pltpu.CompilerParams(vmem_limit_bytes=mib << 20),
        **more,
    )


def per_device(band_tiles, widths, warm_start, scores, penalty):
    n_seg = lax.axis_size("seg")
    tiles = pltpu.with_memory_space_constraint(jnp.transpose(band_tiles[0], (1, 0, 2)), HBM)
    depth, block_len, strip = tiles.shape
    columns = warm_start.shape[1]
    scores_t = scores.T
    pen = jnp.broadcast_to((step_size * penalty)[:, None], (columns, strip))

    def shape(dtype, *lead):
        return jax.ShapeDtypeStruct((*lead, columns, strip), dtype)

    flops = 2 * depth * block_len * strip * columns
    tile_bytes = depth * block_len * strip * 2
    one = columns * strip
    seg_sems = pltpu.SemaphoreType.DMA((n_seg,))
    fresh = (shape(F32), shape(BF16))
    begin = call(
        begin_kernel,
        fresh,
        1,
        0,
        one,
        8 * one,
        4,
        outside=(0,),
        scratch_shapes=[VMEM((2, strip // 2, columns), F32), pltpu.SemaphoreType.DMA((2,))],
    )
    spread = call(
        spread_kernel,
        HBM((n_seg, columns, strip), BF16),
        1,
        0,
        one,
        10 * one,
        2,
        out_outside=(0,),
        scratch_shapes=[seg_sems],
    )
    pair = call(pair_kernel, shape(BF16, 2), 2, 0, one, 8 * one, 2)
    load = call(
        load_kernel,
        jax.ShapeDtypeStruct((EARLY, block_len, strip), BF16),
        2,
        0,
        one,
        tile_bytes * EARLY // depth,
        4,
        outside=(0,),
        scratch_shapes=[pltpu.SemaphoreType.DMA],
    )
    backward = call(
        backward_kernel,
        (
            shape(F32),
            shape(BF16, 3),
            shape(BF16, 6),
            jax.ShapeDtypeStruct((depth - EARLY, block_len, strip), BF16),
        ),
        4,
        1,
        flops,
        tile_bytes,
        8,
        outside=(1,),
        scratch_shapes=[pltpu.SemaphoreType.DMA((depth - EARLY,))],
    )
    lend = call(lend_kernel, shape(BF16, 6), 4, 0, one, 12 * one, 4, input_output_aliases={0: 0})
    forward_even = call(forward_even_kernel, shape(F32, n_seg), 6, 1, flops * 4 // 7, tile_bytes, 8)
    forward_odd = call(
        forward_odd_kernel,
        HBM((n_seg, columns, strip), BF16),
        5,
        1,
        flops * 3 // 7,
        tile_bytes,
        8,
        out_outside=(0,),
        scratch_shapes=[VMEM((n_seg, columns, strip), BF16), seg_sems],
    )
    combine = call(combine_kernel, (shape(BF16, 2), shape(BF16)), 2, 0, one, 18 * one, 4)
    relay = call(relay_kernel, shape(BF16), 2, 0, one, 6 * one, 2)
    settle = call(settle_kernel, shape(F32), 5, 0, one, 14 * one, 4)
    update = call(update_kernel, fresh, 4, 0, one, 12 * one, 6)
    final = call(final_kernel, jax.ShapeDtypeStruct((strip, columns), F32), 4, 0, one, 12 * one, 6)

    estimate, current = begin(pltpu.with_memory_space_constraint(warm_start, HBM))
    for iteration in range(ITERS):
        far = shifted(current, -4)
        copies = spread(current)
        block = lax.all_to_all(copies, "seg", 0, 0)
        near = shifted(pair(current, far), -2)
        early = load(tiles, far)
        first, even, lent, late = backward(widths, tiles, early, block)
        got = swapped(lend(lent, current, near, far))
        total = forward_even(widths, early, late, current, near, far)
        back_pair, mid = combine(even, got)
        back_first = shifted(back_pair, 4)
        partial = forward_odd(widths, early, late, got, total)
        summed = lax.all_to_all(partial, "seg", 0, 0)
        back_last = shifted(relay(mid, back_first), 2)
        settled = settle(estimate, first, got, back_first, scores_t)
        if iteration < ITERS - 1:
            estimate, current = update(settled, summed, back_last, pen)
        else:
            return final(settled, summed, back_last, pen)


def solution(mesh):
    in_specs = (
        P("chain", None, None, "seg"),
        P("chain"),
        P(("chain", "seg"), None),
        P(("chain", "seg"), None),
        P(),
    )
    out_specs = P(("chain", "seg"), None)
    return jax.shard_map(
        per_device, mesh=mesh, in_specs=in_specs, out_specs=out_specs, check_vma=False
    )
```
